768 devices in a mesh: ctx: 96 (over y, z), head: 8 (over x, core).
Axes of the slice: x: 4, y: 8, z: 12, core: 2. Of those that a mesh axis runs over, the one named last changes fastest.
Arguments:
- lin_q: bfloat16 [12288, 4096], P('ctx', 'head'), may hold values from -5 to 5
- lin_k: bfloat16 [12288, 4096], P('ctx', 'head'), may hold values from -5 to 5
- lin_v: bfloat16 [12288, 4096], P('ctx', 'head'), may hold values from -13 to 13
- win_q: bfloat16 [12288, 4096], P('ctx', 'head'), may hold values from -5 to 5
- win_k: bfloat16 [12288, 4096], P('ctx', 'head'), may hold values from -5 to 5
- win_v: bfloat16 [12288, 4096], P('ctx', 'head'), may hold values from -5 to 5
- grad_out: bfloat16 [12288, 4096], P('ctx', 'head'), may hold values from -5 to 5
Outputs:
- mixed: bfloat16 [12288, 4096], P('ctx', 'head')
- grad_lin_q: bfloat16 [12288, 4096], P('ctx', 'head')
- grad_lin_k: bfloat16 [12288, 4096], P('ctx', 'head')
- grad_lin_v: bfloat16 [12288, 4096], P('ctx', 'head')
- grad_win_q: bfloat16 [12288, 4096], P('ctx', 'head')
- grad_win_k: bfloat16 [12288, 4096], P('ctx', 'head')
- grad_win_v: bfloat16 [12288, 4096], P('ctx', 'head')
The draws below stay inside these ranges and needn't reach their ends.
All inputs are finite; a program needn't handle non-finite values.
Results may differ from the reference program's by a relative error of at most 0.0084.
Values may be sent and summed in bfloat16 or wider, within the bound.
No kernel may reach another device: no remote copies, remote signals or barrier semaphores. Data moves between devices by JAX's collectives and lax.ppermute only.
A program may use at most 64 MiB of HBM per device.

```python
import math
import jax
import jax.numpy as jnp
from jax import lax

HD = 128
WIN = 512
TOK_DEV = 128
HEADS = 32
TOKENS = 12288


def drawn_pair(key):
    base = jax.random.fold_in(key, 17)
    key_query, key_keys = jax.random.split(base, 2)
    shape = (TOKENS, HEADS * HD)
    query = jnp.clip(1.4 * jax.random.normal(key_query, shape, jnp.float32), -5.0, 5.0)
    keys = jnp.clip(1.4 * jax.random.normal(key_keys, shape, jnp.float32), -5.0, 5.0)
    return (query, keys)


def draw_win_q(key, part):
    return drawn_pair(key)[0].astype(jnp.bfloat16)


def draw_win_k(key, part):
    return drawn_pair(key)[1].astype(jnp.bfloat16)


def draw_lin_v(key, part):
    base = jax.random.fold_in(key, 29)
    key_body, key_spread = jax.random.split(base, 2)
    columns = HEADS * HD
    feature = jnp.arange(columns, dtype=jnp.float32) / columns
    values = jnp.clip(jax.random.normal(key_body, (TOKENS, columns), jnp.float32), -4.0, 4.0)
    rising = 0.5
    offset = -0.5
    spread = jax.random.uniform(key_spread, (columns,), jnp.float32, 0.0, 0.5)
    column_scale = 10.0 ** (rising * feature + spread + offset)
    return (values * column_scale[None, :]).astype(jnp.bfloat16)


def steps_of(key, shape, shards, low, largest):
    factor_of, own = 1.0, jax.random.fold_in(key, 6)
    for dim, parts in shards:
        steps = jnp.exp(jax.random.uniform(jax.random.fold_in(own, dim), (parts,), jnp.float32, low / len(shards), largest / len(shards)))
        factor_of = factor_of * jnp.repeat(steps, shape[dim] // parts).reshape([-1 if axis == dim else 1 for axis in range(len(shape))])
    return factor_of


def bell_draw(rng, extent, width, reach, shards=(), held_as=jnp.bfloat16):
    values = width * jax.random.normal(rng, extent, jnp.float32)
    if shards:
        values = values * steps_of(rng, extent, shards, -0.22, 0.18)
    return jnp.clip(values, -reach, reach).astype(held_as)


def setup_inputs(seed: int = 0) -> dict:
    key_list = jax.random.split(jax.random.key(seed), 8)
    lin_q = bell_draw(key_list[0], (TOKENS, HEADS * HD), 1.0, 5.0, ((0, 96), (1, 8)))
    lin_k = bell_draw(key_list[1], (TOKENS, HEADS * HD), 1.0, 5.0, ((0, 96), (1, 8)))
    lin_v = draw_lin_v(jax.random.fold_in(key_list[7], 71), 0)
    win_q = draw_win_q(jax.random.fold_in(key_list[7], 71), 0)
    win_k = draw_win_k(jax.random.fold_in(key_list[7], 71), 0)
    win_v = bell_draw(key_list[5], (TOKENS, HEADS * HD), 1.0, 5.0, ((0, 96), (1, 8)))
    grad_out = bell_draw(key_list[6], (TOKENS, HEADS * HD), 1.0, 5.0, ((0, 96), (1, 8)))
    return dict(lin_q=lin_q, lin_k=lin_k, lin_v=lin_v, win_q=win_q, win_k=win_k, win_v=win_v, grad_out=grad_out)


PRECISE = lax.Precision.HIGHEST
NORM_EPS = 1e-05

def split_blocks(array, block_rows):
    return array.reshape((array.shape[0] // block_rows, block_rows) + array.shape[1:])

def block_states(left, right, block_rows):
    first_part = split_blocks(left.astype(jnp.float32), block_rows)
    second_part = split_blocks(right.astype(jnp.float32), block_rows)
    return jnp.einsum('bshd,bshe->bhde', first_part, second_part, precision=PRECISE)

def exclusive(states, reverse):
    empty = jnp.zeros_like(states[:1])
    if reverse:
        running = jnp.cumsum(states[::-1], axis=0)[::-1]
        return jnp.concatenate([running[1:], empty], axis=0)
    running = jnp.cumsum(states, axis=0)
    return jnp.concatenate([empty, running[:-1]], axis=0)

def causal_rows(block_rows):
    positions = jnp.arange(block_rows, dtype=jnp.int32)
    return positions[:, None] >= positions[None, :]

def linear_forward(query, keys, values, before_blocks, block_rows):
    causal = causal_rows(block_rows)

    def per_block(pieces):
        query_f = pieces[0].astype(jnp.float32)
        keys_f = pieces[1].astype(jnp.float32)
        values_f = pieces[2].astype(jnp.float32)
        scores = jnp.einsum('thd,shd->hts', query_f, keys_f, precision=PRECISE)
        scores = jnp.where(causal[None], scores, 0.0)
        inner = jnp.einsum('hts,shd->thd', scores, values_f, precision=PRECISE)
        return inner + jnp.einsum('thd,hde->the', query_f, pieces[3], precision=PRECISE)
    result = lax.map(per_block, (split_blocks(query, block_rows), split_blocks(keys, block_rows), split_blocks(values, block_rows), before_blocks))
    return result.reshape(query.shape)

def linear_backward(query, keys, values, cotangent, before_blocks, after_blocks, block_rows):
    causal = causal_rows(block_rows)

    def per_block(pieces):
        query_f = pieces[0].astype(jnp.float32)
        keys_f = pieces[1].astype(jnp.float32)
        values_f = pieces[2].astype(jnp.float32)
        upstream = pieces[3].astype(jnp.float32)
        scores = jnp.einsum('thd,shd->hts', query_f, keys_f, precision=PRECISE)
        scores = jnp.where(causal[None], scores, 0.0)
        dprobs = jnp.einsum('the,she->hts', upstream, values_f, precision=PRECISE)
        dprobs = jnp.where(causal[None], dprobs, 0.0)
        query_grad = jnp.einsum('hts,shd->thd', dprobs, keys_f, precision=PRECISE)
        query_grad = query_grad + jnp.einsum('the,hde->thd', upstream, pieces[4], precision=PRECISE)
        key_grad = jnp.einsum('hts,thd->shd', dprobs, query_f, precision=PRECISE)
        key_grad = key_grad + jnp.einsum('she,hde->shd', values_f, pieces[5], precision=PRECISE)
        value_grad = jnp.einsum('hts,the->she', scores, upstream, precision=PRECISE)
        value_grad = value_grad + jnp.einsum('shd,hde->she', keys_f, pieces[5], precision=PRECISE)
        return (query_grad, key_grad, value_grad)
    grads = lax.map(per_block, (split_blocks(query, block_rows), split_blocks(keys, block_rows), split_blocks(values, block_rows), split_blocks(cotangent, block_rows), before_blocks, after_blocks))
    return tuple((item.reshape(query.shape) for item in grads))

def query_head(query, keys, values, upstream, first_pos):
    row_count = query.shape[0]
    ext_count = keys.shape[0]
    window = ext_count - row_count
    score_scale = 1.0 / math.sqrt(query.shape[1])
    keys_f = keys.astype(jnp.float32)
    values_f = values.astype(jnp.float32)
    scores = jnp.einsum('td,sd->ts', query.astype(jnp.float32), keys_f, precision=PRECISE) * score_scale
    query_pos = first_pos + jnp.arange(row_count, dtype=jnp.int32)
    key_pos = first_pos - window + jnp.arange(ext_count, dtype=jnp.int32)
    allowed = (key_pos[None, :] >= 0) & (key_pos[None, :] <= query_pos[:, None]) & (key_pos[None, :] > query_pos[:, None] - window)
    scores = jnp.where(allowed, scores, -jnp.inf)
    row_max = lax.optimization_barrier(jnp.max(scores, axis=1, keepdims=True))
    log_total = row_max[:, 0] + jnp.log(lax.optimization_barrier(jnp.sum(jnp.exp(scores - row_max), axis=1)))
    probs = jnp.exp(scores - log_total[:, None])
    weights_low = probs.astype(jnp.bfloat16)
    output = jnp.einsum('ts,sd->td', weights_low.astype(jnp.float32), values_f, precision=PRECISE)
    dprobs = jnp.einsum('td,sd->ts', upstream.astype(jnp.float32), values_f, precision=PRECISE)
    row_dot = lax.optimization_barrier(jnp.sum(probs * dprobs, axis=1))
    dscores = (probs * (dprobs - row_dot[:, None]) * score_scale).astype(jnp.bfloat16)
    query_grad = jnp.einsum('ts,sd->td', dscores.astype(jnp.float32), keys_f, precision=PRECISE)
    return (output, query_grad, log_total, row_dot)

def key_head(query, upstream, totals, dots, keys, values, first_pos, total_rows):
    row_count = keys.shape[0]
    ext_count = query.shape[0]
    window = ext_count - row_count
    score_scale = 1.0 / math.sqrt(query.shape[1])
    query_f = query.astype(jnp.float32)
    upstream_f = upstream.astype(jnp.float32)
    scores = jnp.einsum('td,sd->ts', query_f, keys.astype(jnp.float32), precision=PRECISE) * score_scale
    query_pos = first_pos + jnp.arange(ext_count, dtype=jnp.int32)
    key_pos = first_pos + jnp.arange(row_count, dtype=jnp.int32)
    allowed = (query_pos[:, None] < total_rows) & (key_pos[None, :] <= query_pos[:, None]) & (key_pos[None, :] > query_pos[:, None] - window)
    probs = jnp.where(allowed, jnp.exp(scores - totals[:, None]), 0.0)
    weights_low = probs.astype(jnp.bfloat16)
    dprobs = jnp.einsum('td,sd->ts', upstream_f, values.astype(jnp.float32), precision=PRECISE)
    dscores = (probs * (dprobs - dots[:, None]) * score_scale).astype(jnp.bfloat16)
    key_grad = jnp.einsum('ts,td->sd', dscores.astype(jnp.float32), query_f, precision=PRECISE)
    value_grad = jnp.einsum('ts,td->sd', weights_low.astype(jnp.float32), upstream_f, precision=PRECISE)
    return (key_grad, value_grad)

def reference(lin_q, lin_k, lin_v, win_q, win_k, win_v, grad_out):
    shaped = (TOKENS, HEADS, HD)
    flat = (TOKENS, HEADS * HD)
    lin_query = lin_q.reshape(shaped)
    lin_key = lin_k.reshape(shaped)
    lin_value = lin_v.reshape(shaped)
    before_blocks = exclusive(block_states(lin_key, lin_value, TOK_DEV), False)
    lin_out = linear_forward(lin_query, lin_key, lin_value, before_blocks, TOK_DEV)
    upstream = grad_out.reshape(shaped).astype(jnp.float32)
    features = HEADS * HD
    square_sum = lax.optimization_barrier(jnp.sum(lin_out * lin_out, axis=(1, 2)))
    cross_sum = lax.optimization_barrier(jnp.sum(upstream * lin_out, axis=(1, 2)))
    inv_rms = lax.rsqrt(square_sum / features + NORM_EPS)
    lin_dout = (inv_rms[:, None, None] * upstream - lin_out * (inv_rms ** 3 * cross_sum / features)[:, None, None]).astype(jnp.bfloat16)
    after_blocks = exclusive(block_states(lin_query, lin_dout, TOK_DEV), True)
    grad_q, grad_k, grad_v = linear_backward(lin_query, lin_key, lin_value, lin_dout, before_blocks, after_blocks, TOK_DEV)
    win_query = win_q.reshape(shaped)
    win_key = win_k.reshape(shaped)
    win_value = win_v.reshape(shaped)
    cotangent = grad_out.reshape(shaped)
    padding = jnp.zeros((WIN, HEADS, HD), jnp.bfloat16)
    key_pad = jnp.concatenate([padding, win_key], axis=0)
    value_pad = jnp.concatenate([padding, win_value], axis=0)
    query_pad = jnp.concatenate([win_query, padding], axis=0)
    upstream_pad = jnp.concatenate([cotangent, padding], axis=0)
    block_index = jnp.arange(TOKENS // TOK_DEV, dtype=jnp.int32)

    def query_block(block):
        first_pos = (block * TOK_DEV).astype(jnp.int32)
        pieces = (lax.dynamic_slice_in_dim(win_query, first_pos, TOK_DEV, 0), lax.dynamic_slice_in_dim(key_pad, first_pos, WIN + TOK_DEV, 0), lax.dynamic_slice_in_dim(value_pad, first_pos, WIN + TOK_DEV, 0), lax.dynamic_slice_in_dim(cotangent, first_pos, TOK_DEV, 0))
        mapped = jax.vmap(lambda a, b, c, d: query_head(a, b, c, d, first_pos), in_axes=1, out_axes=(1, 1, 0, 0))
        return mapped(*pieces)
    win_out, win_dq, log_total, row_dot = lax.map(query_block, block_index)
    win_out = win_out.reshape(shaped)
    win_dq = win_dq.reshape(shaped)
    stat_pad = jnp.zeros((HEADS, WIN), jnp.float32)
    total_all = jnp.concatenate([jnp.moveaxis(log_total, 0, 1).reshape(HEADS, TOKENS), stat_pad], axis=1)
    dot_all = jnp.concatenate([jnp.moveaxis(row_dot, 0, 1).reshape(HEADS, TOKENS), stat_pad], axis=1)

    def key_block(block):
        first_pos = (block * TOK_DEV).astype(jnp.int32)
        pieces = (lax.dynamic_slice_in_dim(query_pad, first_pos, WIN + TOK_DEV, 0), lax.dynamic_slice_in_dim(upstream_pad, first_pos, WIN + TOK_DEV, 0), lax.dynamic_slice_in_dim(total_all, first_pos, WIN + TOK_DEV, 1), lax.dynamic_slice_in_dim(dot_all, first_pos, WIN + TOK_DEV, 1), lax.dynamic_slice_in_dim(win_key, first_pos, TOK_DEV, 0), lax.dynamic_slice_in_dim(win_value, first_pos, TOK_DEV, 0))
        mapped = jax.vmap(lambda a, b, c, d, e, f: key_head(a, b, c, d, e, f, first_pos, TOKENS), in_axes=(1, 1, 0, 0, 1, 1), out_axes=(1, 1))
        return mapped(*pieces)
    win_dk, win_dv = lax.map(key_block, block_index)
    mixed = (lin_out * inv_rms[:, None, None] + win_out).astype(jnp.bfloat16).reshape(flat)
    return (mixed, grad_q.astype(jnp.bfloat16).reshape(flat), grad_k.astype(jnp.bfloat16).reshape(flat), grad_v.astype(jnp.bfloat16).reshape(flat), win_dq.astype(jnp.bfloat16).reshape(flat), win_dk.astype(jnp.bfloat16).reshape(flat), win_dv.astype(jnp.bfloat16).reshape(flat))
```

```python
import math

import jax
import jax.numpy as jnp
from jax import lax
from jax.sharding import PartitionSpec as P

HD = 128
WIN = 512
LANES = 128


PRECISE = lax.Precision.HIGHEST
NORM_EPS = 1e-05


def scan_states(state, axis, reverse):
    count = lax.axis_size(axis)
    flat = state.reshape(-1, LANES)
    rows = flat.shape[0]
    per = -(-rows // count)
    flat = jnp.pad(flat, ((0, per * count - rows), (0, 0)))
    pieces = flat.reshape(count, per * LANES)
    gathered = lax.all_to_all(pieces, axis, 0, 0, tiled=True)
    index = jnp.arange(count, dtype=jnp.int32)
    if reverse:
        mask = index[None, :] > index[:, None]
    else:
        mask = index[None, :] < index[:, None]
    sums = jnp.einsum(
        "ij,jf->if", mask.astype(jnp.float32), gathered, precision=PRECISE
    )
    returned = lax.all_to_all(sums, axis, 0, 0, tiled=True)
    return returned.reshape(count * per, LANES)[:rows].reshape(state.shape)


def passed_along(block, axis, distance):
    devices = range(lax.axis_size(axis))
    route = [(i - distance, i) for i in devices if i - distance in devices]
    return lax.ppermute(block, axis, route)


def causal_rows(block_rows):
    positions = jnp.arange(block_rows, dtype=jnp.int32)
    return positions[:, None] >= positions[None, :]


def linear_forward(query, keys, values, before):
    causal = causal_rows(query.shape[0])
    scores = jnp.einsum("thd,shd->hts", query, keys, preferred_element_type=jnp.float32)
    scores = jnp.where(causal[None], scores, 0.0)
    inner = jnp.einsum("hts,shd->thd", scores, values.astype(jnp.float32), precision=PRECISE)
    result = inner + jnp.einsum(
        "thd,hde->the", query.astype(jnp.float32), before, precision=PRECISE
    )
    return (result, scores)


def linear_backward(query, keys, values, cotangent, scores, before, after):
    causal = causal_rows(query.shape[0])
    cotangent_f = cotangent.astype(jnp.float32)
    dprobs = jnp.einsum("the,she->hts", cotangent, values, preferred_element_type=jnp.float32)
    dprobs = jnp.where(causal[None], dprobs, 0.0)
    query_grad = jnp.einsum("hts,shd->thd", dprobs, keys.astype(jnp.float32), precision=PRECISE)
    query_grad = query_grad + jnp.einsum("the,hde->thd", cotangent_f, before, precision=PRECISE)
    key_grad = jnp.einsum("hts,thd->shd", dprobs, query.astype(jnp.float32), precision=PRECISE)
    key_grad = key_grad + jnp.einsum(
        "she,hde->shd", values.astype(jnp.float32), after, precision=PRECISE
    )
    value_grad = jnp.einsum("hts,the->she", scores, cotangent_f, precision=PRECISE)
    value_grad = value_grad + jnp.einsum(
        "shd,hde->she", keys.astype(jnp.float32), after, precision=PRECISE
    )
    return (query_grad, key_grad, value_grad)


def query_head(query, keys, values, upstream, first_pos):
    row_count = query.shape[0]
    ext_count = keys.shape[0]
    window = ext_count - row_count
    score_scale = 1.0 / math.sqrt(query.shape[2])
    scores = jnp.einsum("thd,shd->hts", query, keys, preferred_element_type=jnp.float32) * score_scale
    query_pos = first_pos + jnp.arange(row_count, dtype=jnp.int32)
    key_pos = first_pos - window + jnp.arange(ext_count, dtype=jnp.int32)
    allowed = (
        (key_pos[None, :] >= 0)
        & (key_pos[None, :] <= query_pos[:, None])
        & (key_pos[None, :] > query_pos[:, None] - window)
    )
    scores = jnp.where(allowed[None], scores, -jnp.inf)
    row_max = jnp.max(scores, axis=2, keepdims=True)
    log_total = row_max[:, :, 0] + jnp.log(jnp.sum(jnp.exp(scores - row_max), axis=2))
    probs = jnp.exp(scores - log_total[:, :, None])
    weights_low = probs.astype(jnp.bfloat16)
    output = jnp.einsum("hts,shd->thd", weights_low, values, preferred_element_type=jnp.float32)
    dprobs = jnp.einsum("thd,shd->hts", upstream, values, preferred_element_type=jnp.float32)
    row_dot = jnp.sum(probs * dprobs, axis=2)
    dscores = (probs * (dprobs - row_dot[:, :, None]) * score_scale).astype(jnp.bfloat16)
    query_grad = jnp.einsum("hts,shd->thd", dscores, keys, preferred_element_type=jnp.float32)
    return (output, query_grad, log_total, row_dot)


def key_head(query, upstream, totals, dots, keys, values, first_pos, total_rows):
    row_count = keys.shape[0]
    ext_count = query.shape[0]
    window = ext_count - row_count
    score_scale = 1.0 / math.sqrt(query.shape[2])
    scores = jnp.einsum("thd,shd->hts", query, keys, preferred_element_type=jnp.float32) * score_scale
    query_pos = first_pos + jnp.arange(ext_count, dtype=jnp.int32)
    key_pos = first_pos + jnp.arange(row_count, dtype=jnp.int32)
    allowed = (
        (query_pos[:, None] < total_rows)
        & (key_pos[None, :] <= query_pos[:, None])
        & (key_pos[None, :] > query_pos[:, None] - window)
    )
    probs = jnp.where(allowed[None], jnp.exp(scores - totals[:, :, None]), 0.0)
    weights_low = probs.astype(jnp.bfloat16)
    dprobs = jnp.einsum("thd,shd->hts", upstream, values, preferred_element_type=jnp.float32)
    dscores = (probs * (dprobs - dots[:, :, None]) * score_scale).astype(jnp.bfloat16)
    key_grad = jnp.einsum("hts,thd->shd", dscores, query, preferred_element_type=jnp.float32)
    value_grad = jnp.einsum("hts,thd->shd", weights_low, upstream, preferred_element_type=jnp.float32)
    return (key_grad, value_grad)


def shards(lin_q, lin_k, lin_v, win_q, win_k, win_v, grad_out):
    row_count = lin_q.shape[0]
    head_count = lin_q.shape[1] // HD
    shaped = (row_count, head_count, HD)
    flat = (row_count, head_count * HD)
    span = WIN // row_count
    total_rows = row_count * lax.axis_size("ctx")
    first_pos = lax.axis_index("ctx") * row_count
    win_query = win_q.reshape(shaped)
    win_key = win_k.reshape(shaped)
    win_value = win_v.reshape(shaped)
    cotangent = grad_out.reshape(shaped)

    earlier_keys, earlier_values = [], []
    later_queries, later_upstreams = [], []
    key_pair = (win_key, win_value)
    row_pair = (win_query, cotangent)
    for _ in range(span):
        key_pair = passed_along(key_pair, "ctx", 1)
        row_pair = passed_along(row_pair, "ctx", -1)
        earlier_keys.insert(0, key_pair[0])
        earlier_values.insert(0, key_pair[1])
        later_queries.append(row_pair[0])
        later_upstreams.append(row_pair[1])

    lin_query = lin_q.reshape(shaped)
    lin_key = lin_k.reshape(shaped)
    lin_value = lin_v.reshape(shaped)
    key_state = jnp.einsum("shd,she->hde", lin_key, lin_value, preferred_element_type=jnp.float32)
    prefix = scan_states(key_state, "ctx", False)
    lin_out, lin_scores = linear_forward(lin_query, lin_key, lin_value, prefix)
    upstream = grad_out.reshape(shaped).astype(jnp.float32)
    square_sum, cross_sum = lax.psum(
        (jnp.sum(lin_out * lin_out, axis=(1, 2)), jnp.sum(upstream * lin_out, axis=(1, 2))), "head"
    )
    features = head_count * HD * lax.axis_size("head")
    inv_rms = lax.rsqrt(square_sum / features + NORM_EPS)
    lin_dout = (
        inv_rms[:, None, None] * upstream
        - lin_out * (inv_rms**3 * cross_sum / features)[:, None, None]
    ).astype(jnp.bfloat16)
    query_state = jnp.einsum(
        "thd,the->hde", lin_query, lin_dout, preferred_element_type=jnp.float32
    )
    suffix = scan_states(query_state, "ctx", True)
    grad_q, grad_k, grad_v = linear_backward(
        lin_query, lin_key, lin_value, lin_dout, lin_scores, prefix, suffix
    )

    key_ext = jnp.concatenate(earlier_keys + [win_key], axis=0)
    value_ext = jnp.concatenate(earlier_values + [win_value], axis=0)
    win_out, win_dq, log_total, row_dot = query_head(
        win_query, key_ext, value_ext, cotangent, first_pos
    )

    later_totals, later_dots = [], []
    stat_pair = (log_total, row_dot)
    for _ in range(span):
        stat_pair = passed_along(stat_pair, "ctx", -1)
        later_totals.append(stat_pair[0])
        later_dots.append(stat_pair[1])
    query_ext = jnp.concatenate([win_query] + later_queries, axis=0)
    upstream_ext = jnp.concatenate([cotangent] + later_upstreams, axis=0)
    total_ext = jnp.concatenate([log_total] + later_totals, axis=1)
    dot_ext = jnp.concatenate([row_dot] + later_dots, axis=1)
    win_dk, win_dv = key_head(
        query_ext, upstream_ext, total_ext, dot_ext, win_key, win_value, first_pos, total_rows
    )
    mixed = (lin_out * inv_rms[:, None, None] + win_out).astype(jnp.bfloat16).reshape(flat)
    return (
        mixed,
        grad_q.astype(jnp.bfloat16).reshape(flat),
        grad_k.astype(jnp.bfloat16).reshape(flat),
        grad_v.astype(jnp.bfloat16).reshape(flat),
        win_dq.astype(jnp.bfloat16).reshape(flat),
        win_dk.astype(jnp.bfloat16).reshape(flat),
        win_dv.astype(jnp.bfloat16).reshape(flat),
    )


def solution(mesh):
    spec = P("ctx", "head")
    return jax.shard_map(
        shards,
        mesh=mesh,
        in_specs=(spec,) * 7,
        out_specs=(spec,) * 7,
        check_vma=False,
    )
```

```python
import math

import jax
import jax.numpy as jnp
from jax import lax
from jax.sharding import PartitionSpec as P

HD = 128
WIN = 512
LANES = 128


PRECISE = lax.Precision.HIGHEST
NORM_EPS = 1e-05


def exclusive_sum(gathered, reverse):
    count = gathered.shape[0]
    index = jnp.arange(count, dtype=jnp.int32)
    if reverse:
        mask = index[None, :] > index[:, None]
    else:
        mask = index[None, :] < index[:, None]
    return jnp.einsum("ij,jf->if", mask.astype(jnp.float32), gathered, precision=PRECISE)


def padded_pieces(vector, count):
    per = -(-vector.shape[0] // count)
    return jnp.pad(vector, (0, per * count - vector.shape[0])).reshape(count, per)


def scan_states(state, outer, inner, reverse):
    flat = state.reshape(-1)
    pieces = padded_pieces(flat, lax.axis_size(inner))
    gathered = lax.all_to_all(pieces, inner, 0, 0, tiled=True)
    within = exclusive_sum(gathered, reverse)
    group_total = jnp.sum(gathered, axis=0)
    parts = padded_pieces(group_total, lax.axis_size(outer))
    gathered_totals = lax.all_to_all(parts, outer, 0, 0, tiled=True)
    across = lax.all_to_all(exclusive_sum(gathered_totals, reverse), outer, 0, 0, tiled=True)
    across = across.reshape(-1)[: group_total.shape[0]]
    returned = lax.all_to_all(within + across[None, :], inner, 0, 0, tiled=True)
    return returned.reshape(-1)[: flat.shape[0]].reshape(state.shape)


def head_sum(values, axis):
    count = lax.axis_size(axis)
    copies = jnp.broadcast_to(values[None], (count,) + values.shape)
    return jnp.sum(lax.all_to_all(copies, axis, 0, 0, tiled=True), axis=0)


def passed_along(block, axis, distance):
    devices = range(lax.axis_size(axis[0]) * lax.axis_size(axis[1]))
    route = [(i - distance, i) for i in devices if i - distance in devices]
    return lax.ppermute(block, axis, route)


def causal_rows(block_rows):
    positions = jnp.arange(block_rows, dtype=jnp.int32)
    return positions[:, None] >= positions[None, :]


def linear_forward(query, keys, values, before):
    causal = causal_rows(query.shape[0])
    scores = jnp.einsum("thd,shd->hts", query, keys, preferred_element_type=jnp.float32)
    scores = jnp.where(causal[None], scores, 0.0)
    inner = jnp.einsum("hts,shd->thd", scores, values.astype(jnp.float32), precision=PRECISE)
    result = inner + jnp.einsum(
        "thd,hde->the", query.astype(jnp.float32), before, precision=PRECISE
    )
    return (result, scores)


def linear_backward(query, keys, values, cotangent, scores, before, after):
    causal = causal_rows(query.shape[0])
    cotangent_f = cotangent.astype(jnp.float32)
    dprobs = jnp.einsum("the,she->hts", cotangent, values, preferred_element_type=jnp.float32)
    dprobs = jnp.where(causal[None], dprobs, 0.0)
    query_grad = jnp.einsum("hts,shd->thd", dprobs, keys.astype(jnp.float32), precision=PRECISE)
    query_grad = query_grad + jnp.einsum("the,hde->thd", cotangent_f, before, precision=PRECISE)
    key_grad = jnp.einsum("hts,thd->shd", dprobs, query.astype(jnp.float32), precision=PRECISE)
    key_grad = key_grad + jnp.einsum(
        "she,hde->shd", values.astype(jnp.float32), after, precision=PRECISE
    )
    value_grad = jnp.einsum("hts,the->she", scores, cotangent_f, precision=PRECISE)
    value_grad = value_grad + jnp.einsum(
        "shd,hde->she", keys.astype(jnp.float32), after, precision=PRECISE
    )
    return (query_grad, key_grad, value_grad)


def query_head(query, keys, values, upstream, first_pos):
    row_count = query.shape[0]
    ext_count = keys.shape[0]
    window = ext_count - row_count
    score_scale = 1.0 / math.sqrt(query.shape[2])
    scores = jnp.einsum("thd,shd->hts", query, keys, preferred_element_type=jnp.float32) * score_scale
    query_pos = first_pos + jnp.arange(row_count, dtype=jnp.int32)
    key_pos = first_pos - window + jnp.arange(ext_count, dtype=jnp.int32)
    allowed = (
        (key_pos[None, :] >= 0)
        & (key_pos[None, :] <= query_pos[:, None])
        & (key_pos[None, :] > query_pos[:, None] - window)
    )
    scores = jnp.where(allowed[None], scores, -jnp.inf)
    row_max = jnp.max(scores, axis=2, keepdims=True)
    log_total = row_max[:, :, 0] + jnp.log(jnp.sum(jnp.exp(scores - row_max), axis=2))
    probs = jnp.exp(scores - log_total[:, :, None])
    weights_low = probs.astype(jnp.bfloat16)
    output = jnp.einsum("hts,shd->thd", weights_low, values, preferred_element_type=jnp.float32)
    dprobs = jnp.einsum("thd,shd->hts", upstream, values, preferred_element_type=jnp.float32)
    row_dot = jnp.sum(probs * dprobs, axis=2)
    dscores = (probs * (dprobs - row_dot[:, :, None]) * score_scale).astype(jnp.bfloat16)
    query_grad = jnp.einsum("hts,shd->thd", dscores, keys, preferred_element_type=jnp.float32)
    return (output, query_grad, log_total, row_dot)


def key_head(query, upstream, totals, dots, keys, values, first_pos, total_rows):
    row_count = keys.shape[0]
    ext_count = query.shape[0]
    window = ext_count - row_count
    score_scale = 1.0 / math.sqrt(query.shape[2])
    scores = jnp.einsum("thd,shd->hts", query, keys, preferred_element_type=jnp.float32) * score_scale
    query_pos = first_pos + jnp.arange(ext_count, dtype=jnp.int32)
    key_pos = first_pos + jnp.arange(row_count, dtype=jnp.int32)
    allowed = (
        (query_pos[:, None] < total_rows)
        & (key_pos[None, :] <= query_pos[:, None])
        & (key_pos[None, :] > query_pos[:, None] - window)
    )
    probs = jnp.where(allowed[None], jnp.exp(scores - totals[:, :, None]), 0.0)
    weights_low = probs.astype(jnp.bfloat16)
    dprobs = jnp.einsum("thd,shd->hts", upstream, values, preferred_element_type=jnp.float32)
    dscores = (probs * (dprobs - dots[:, :, None]) * score_scale).astype(jnp.bfloat16)
    key_grad = jnp.einsum("hts,thd->shd", dscores, query, preferred_element_type=jnp.float32)
    value_grad = jnp.einsum("hts,thd->shd", weights_low, upstream, preferred_element_type=jnp.float32)
    return (key_grad, value_grad)


CTX = ("cy", "cz")


def shards(lin_q, lin_k, lin_v, win_q, win_k, win_v, grad_out):
    row_count = lin_q.shape[0]
    head_count = lin_q.shape[1] // HD
    shaped = (row_count, head_count, HD)
    flat = (row_count, head_count * HD)
    span = WIN // row_count
    total_rows = row_count * lax.axis_size(CTX[0]) * lax.axis_size(CTX[1])
    first_pos = lax.axis_index(CTX) * row_count
    win_query = win_q.reshape(shaped)
    win_key = win_k.reshape(shaped)
    win_value = win_v.reshape(shaped)
    cotangent = grad_out.reshape(shaped)

    earlier_keys, earlier_values = [], []
    later_queries, later_upstreams = [], []
    key_pair = jnp.stack([win_key, win_value])
    row_pair = jnp.stack([win_query, cotangent])
    for _ in range(span):
        key_pair = passed_along(key_pair, CTX, 1)
        row_pair = passed_along(row_pair, CTX, -1)
        earlier_keys.insert(0, key_pair[0])
        earlier_values.insert(0, key_pair[1])
        later_queries.append(row_pair[0])
        later_upstreams.append(row_pair[1])

    lin_query = lin_q.reshape(shaped)
    lin_key = lin_k.reshape(shaped)
    lin_value = lin_v.reshape(shaped)
    key_state = jnp.einsum("shd,she->hde", lin_key, lin_value, preferred_element_type=jnp.float32)
    prefix = scan_states(key_state, CTX[0], CTX[1], False)
    lin_out, lin_scores = linear_forward(lin_query, lin_key, lin_value, prefix)
    upstream = grad_out.reshape(shaped).astype(jnp.float32)
    square_sum, cross_sum = head_sum(
        jnp.stack([jnp.sum(lin_out * lin_out, axis=(1, 2)), jnp.sum(upstream * lin_out, axis=(1, 2))]),
        "head",
    )
    features = head_count * HD * lax.axis_size("head")
    inv_rms = lax.rsqrt(square_sum / features + NORM_EPS)
    lin_dout = (
        inv_rms[:, None, None] * upstream
        - lin_out * (inv_rms**3 * cross_sum / features)[:, None, None]
    ).astype(jnp.bfloat16)
    query_state = jnp.einsum(
        "thd,the->hde", lin_query, lin_dout, preferred_element_type=jnp.float32
    )
    suffix = scan_states(query_state, CTX[0], CTX[1], True)
    grad_q, grad_k, grad_v = linear_backward(
        lin_query, lin_key, lin_value, lin_dout, lin_scores, prefix, suffix
    )

    key_ext = jnp.concatenate(earlier_keys + [win_key], axis=0)
    value_ext = jnp.concatenate(earlier_values + [win_value], axis=0)
    win_out, win_dq, log_total, row_dot = query_head(
        win_query, key_ext, value_ext, cotangent, first_pos
    )

    later_totals, later_dots = [], []
    stat_pair = jnp.stack([log_total, row_dot])
    for _ in range(span):
        stat_pair = passed_along(stat_pair, CTX, -1)
        later_totals.append(stat_pair[0])
        later_dots.append(stat_pair[1])
    query_ext = jnp.concatenate([win_query] + later_queries, axis=0)
    upstream_ext = jnp.concatenate([cotangent] + later_upstreams, axis=0)
    total_ext = jnp.concatenate([log_total] + later_totals, axis=1)
    dot_ext = jnp.concatenate([row_dot] + later_dots, axis=1)
    win_dk, win_dv = key_head(
        query_ext, upstream_ext, total_ext, dot_ext, win_key, win_value, first_pos, total_rows
    )
    mixed = (lin_out * inv_rms[:, None, None] + win_out).astype(jnp.bfloat16).reshape(flat)
    return (
        mixed,
        grad_q.astype(jnp.bfloat16).reshape(flat),
        grad_k.astype(jnp.bfloat16).reshape(flat),
        grad_v.astype(jnp.bfloat16).reshape(flat),
        win_dq.astype(jnp.bfloat16).reshape(flat),
        win_dk.astype(jnp.bfloat16).reshape(flat),
        win_dv.astype(jnp.bfloat16).reshape(flat),
    )


def ctx_groups(mesh):
    column = list(mesh.devices[:, 0])
    count = len(column)
    try:
        slow = [tuple(d.coords)[1] for d in column]
    except (AttributeError, TypeError, IndexError):
        return 1, count
    inner = next((i for i, y in enumerate(slow) if y != slow[0]), count)
    if count % inner:
        inner = count
    return count // inner, inner


def solution(mesh):
    outer, inner = ctx_groups(mesh)
    heads = mesh.devices.shape[1]
    split = jax.sharding.Mesh(mesh.devices.reshape(outer, inner, heads), CTX + ("head",))
    spec = P(CTX, "head")
    return jax.shard_map(
        shards,
        mesh=split,
        in_specs=(spec,) * 7,
        out_specs=(spec,) * 7,
        check_vma=False,
    )
```

```python
import math

import jax
import jax.numpy as jnp
from jax import lax
from jax.sharding import PartitionSpec as P

HD = 128
WIN = 512
LANES = 128


PRECISE = lax.Precision.HIGHEST
NORM_EPS = 1e-05


def exclusive_sum(gathered, reverse):
    count = gathered.shape[0]
    index = jnp.arange(count, dtype=jnp.int32)
    if reverse:
        mask = index[None, :] > index[:, None]
    else:
        mask = index[None, :] < index[:, None]
    return jnp.einsum("ij,jf->if", mask.astype(jnp.float32), gathered, precision=PRECISE)


def padded_pieces(vector, count):
    per = -(-vector.shape[0] // count)
    return jnp.pad(vector, (0, per * count - vector.shape[0])).reshape(count, per)


def scan_states(state, outer, inner, reverse):
    flat = state.reshape(-1)
    pieces = padded_pieces(flat, lax.axis_size(inner))
    gathered = lax.all_to_all(pieces, inner, 0, 0, tiled=True)
    within = exclusive_sum(gathered, reverse)
    group_total = jnp.sum(gathered, axis=0)
    groups = lax.axis_size(outer)
    copies = jnp.broadcast_to(group_total[None], (groups,) + group_total.shape)
    gathered_totals = lax.all_to_all(copies, outer, 0, 0, tiled=True)
    index = jnp.arange(groups, dtype=jnp.int32)
    mine = lax.axis_index(outer)
    chosen = (index > mine) if reverse else (index < mine)
    across = jnp.einsum(
        "j,jf->f", chosen.astype(jnp.float32), gathered_totals, precision=PRECISE
    )
    returned = lax.all_to_all(within + across[None, :], inner, 0, 0, tiled=True)
    return returned.reshape(-1)[: flat.shape[0]].reshape(state.shape)


def head_sum(values, axis):
    count = lax.axis_size(axis)
    copies = jnp.broadcast_to(values[None], (count,) + values.shape)
    return jnp.sum(lax.all_to_all(copies, axis, 0, 0, tiled=True), axis=0)


def passed_along(block, axis, distance):
    devices = range(lax.axis_size(axis[0]) * lax.axis_size(axis[1]))
    route = [(i - distance, i) for i in devices if i - distance in devices]
    return lax.ppermute(block, axis, route)


def causal_rows(block_rows):
    positions = jnp.arange(block_rows, dtype=jnp.int32)
    return positions[:, None] >= positions[None, :]


def linear_forward(query, keys, values, before):
    causal = causal_rows(query.shape[0])
    scores = jnp.einsum("thd,shd->hts", query, keys, preferred_element_type=jnp.float32)
    scores = jnp.where(causal[None], scores, 0.0)
    inner = jnp.einsum("hts,shd->thd", scores, values.astype(jnp.float32), precision=PRECISE)
    result = inner + jnp.einsum(
        "thd,hde->the", query.astype(jnp.float32), before, precision=PRECISE
    )
    return (result, scores)


def linear_backward(query, keys, values, cotangent, scores, before, after):
    causal = causal_rows(query.shape[0])
    cotangent_f = cotangent.astype(jnp.float32)
    dprobs = jnp.einsum("the,she->hts", cotangent, values, preferred_element_type=jnp.float32)
    dprobs = jnp.where(causal[None], dprobs, 0.0)
    query_grad = jnp.einsum("hts,shd->thd", dprobs, keys.astype(jnp.float32), precision=PRECISE)
    query_grad = query_grad + jnp.einsum("the,hde->thd", cotangent_f, before, precision=PRECISE)
    key_grad = jnp.einsum("hts,thd->shd", dprobs, query.astype(jnp.float32), precision=PRECISE)
    key_grad = key_grad + jnp.einsum(
        "she,hde->shd", values.astype(jnp.float32), after, precision=PRECISE
    )
    value_grad = jnp.einsum("hts,the->she", scores, cotangent_f, precision=PRECISE)
    value_grad = value_grad + jnp.einsum(
        "shd,hde->she", keys.astype(jnp.float32), after, precision=PRECISE
    )
    return (query_grad, key_grad, value_grad)


def query_head(query, keys, values, upstream, first_pos):
    row_count = query.shape[0]
    ext_count = keys.shape[0]
    window = ext_count - row_count
    score_scale = 1.0 / math.sqrt(query.shape[2])
    scores = jnp.einsum("thd,shd->hts", query, keys, preferred_element_type=jnp.float32) * score_scale
    query_pos = first_pos + jnp.arange(row_count, dtype=jnp.int32)
    key_pos = first_pos - window + jnp.arange(ext_count, dtype=jnp.int32)
    allowed = (
        (key_pos[None, :] >= 0)
        & (key_pos[None, :] <= query_pos[:, None])
        & (key_pos[None, :] > query_pos[:, None] - window)
    )
    scores = jnp.where(allowed[None], scores, -jnp.inf)
    row_max = jnp.max(scores, axis=2, keepdims=True)
    log_total = row_max[:, :, 0] + jnp.log(jnp.sum(jnp.exp(scores - row_max), axis=2))
    probs = jnp.exp(scores - log_total[:, :, None])
    weights_low = probs.astype(jnp.bfloat16)
    output = jnp.einsum("hts,shd->thd", weights_low, values, preferred_element_type=jnp.float32)
    dprobs = jnp.einsum("thd,shd->hts", upstream, values, preferred_element_type=jnp.float32)
    row_dot = jnp.sum(probs * dprobs, axis=2)
    dscores = (probs * (dprobs - row_dot[:, :, None]) * score_scale).astype(jnp.bfloat16)
    query_grad = jnp.einsum("hts,shd->thd", dscores, keys, preferred_element_type=jnp.float32)
    return (output, query_grad, log_total, row_dot)


def key_head(query, upstream, totals, dots, keys, values, first_pos, total_rows):
    row_count = keys.shape[0]
    ext_count = query.shape[0]
    window = ext_count - row_count
    score_scale = 1.0 / math.sqrt(query.shape[2])
    scores = jnp.einsum("thd,shd->hts", query, keys, preferred_element_type=jnp.float32) * score_scale
    query_pos = first_pos + jnp.arange(ext_count, dtype=jnp.int32)
    key_pos = first_pos + jnp.arange(row_count, dtype=jnp.int32)
    allowed = (
        (query_pos[:, None] < total_rows)
        & (key_pos[None, :] <= query_pos[:, None])
        & (key_pos[None, :] > query_pos[:, None] - window)
    )
    probs = jnp.where(allowed[None], jnp.exp(scores - totals[:, :, None]), 0.0)
    weights_low = probs.astype(jnp.bfloat16)
    dprobs = jnp.einsum("thd,shd->hts", upstream, values, preferred_element_type=jnp.float32)
    dscores = (probs * (dprobs - dots[:, :, None]) * score_scale).astype(jnp.bfloat16)
    key_grad = jnp.einsum("hts,thd->shd", dscores, query, preferred_element_type=jnp.float32)
    value_grad = jnp.einsum("hts,thd->shd", weights_low, upstream, preferred_element_type=jnp.float32)
    return (key_grad, value_grad)


CTX = ("cy", "cz")


def shards(lin_q, lin_k, lin_v, win_q, win_k, win_v, grad_out):
    row_count = lin_q.shape[0]
    head_count = lin_q.shape[1] // HD
    shaped = (row_count, head_count, HD)
    flat = (row_count, head_count * HD)
    span = WIN // row_count
    total_rows = row_count * lax.axis_size(CTX[0]) * lax.axis_size(CTX[1])
    first_pos = lax.axis_index(CTX) * row_count
    win_query = win_q.reshape(shaped)
    win_key = win_k.reshape(shaped)
    win_value = win_v.reshape(shaped)
    cotangent = grad_out.reshape(shaped)

    earlier_keys, earlier_values = [], []
    later_queries, later_upstreams = [], []
    key_pair = jnp.stack([win_key, win_value])
    row_pair = jnp.stack([win_query, cotangent])
    for _ in range(span):
        key_pair = passed_along(key_pair, CTX, 1)
        row_pair = passed_along(row_pair, CTX, -1)
        earlier_keys.insert(0, key_pair[0])
        earlier_values.insert(0, key_pair[1])
        later_queries.append(row_pair[0])
        later_upstreams.append(row_pair[1])

    lin_query = lin_q.reshape(shaped)
    lin_key = lin_k.reshape(shaped)
    lin_value = lin_v.reshape(shaped)
    key_state = jnp.einsum("shd,she->hde", lin_key, lin_value, preferred_element_type=jnp.float32)
    prefix = scan_states(key_state, CTX[0], CTX[1], False)
    lin_out, lin_scores = linear_forward(lin_query, lin_key, lin_value, prefix)
    upstream = grad_out.reshape(shaped).astype(jnp.float32)
    square_sum, cross_sum = head_sum(
        jnp.stack([jnp.sum(lin_out * lin_out, axis=(1, 2)), jnp.sum(upstream * lin_out, axis=(1, 2))]),
        "head",
    )
    features = head_count * HD * lax.axis_size("head")
    inv_rms = lax.rsqrt(square_sum / features + NORM_EPS)
    lin_dout = (
        inv_rms[:, None, None] * upstream
        - lin_out * (inv_rms**3 * cross_sum / features)[:, None, None]
    ).astype(jnp.bfloat16)
    query_state = jnp.einsum(
        "thd,the->hde", lin_query, lin_dout, preferred_element_type=jnp.float32
    )
    suffix = scan_states(query_state, CTX[0], CTX[1], True)
    grad_q, grad_k, grad_v = linear_backward(
        lin_query, lin_key, lin_value, lin_dout, lin_scores, prefix, suffix
    )

    key_ext = jnp.concatenate(earlier_keys + [win_key], axis=0)
    value_ext = jnp.concatenate(earlier_values + [win_value], axis=0)
    win_out, win_dq, log_total, row_dot = query_head(
        win_query, key_ext, value_ext, cotangent, first_pos
    )

    later_totals, later_dots = [], []
    stat_pair = jnp.stack([log_total, row_dot])
    for distance in range(1, span + 1):
        stat_pair = passed_along(jnp.stack([log_total, row_dot]), CTX, -distance)
        later_totals.append(stat_pair[0])
        later_dots.append(stat_pair[1])
    query_ext = jnp.concatenate([win_query] + later_queries, axis=0)
    upstream_ext = jnp.concatenate([cotangent] + later_upstreams, axis=0)
    total_ext = jnp.concatenate([log_total] + later_totals, axis=1)
    dot_ext = jnp.concatenate([row_dot] + later_dots, axis=1)
    win_dk, win_dv = key_head(
        query_ext, upstream_ext, total_ext, dot_ext, win_key, win_value, first_pos, total_rows
    )
    mixed = (lin_out * inv_rms[:, None, None] + win_out).astype(jnp.bfloat16).reshape(flat)
    return (
        mixed,
        grad_q.astype(jnp.bfloat16).reshape(flat),
        grad_k.astype(jnp.bfloat16).reshape(flat),
        grad_v.astype(jnp.bfloat16).reshape(flat),
        win_dq.astype(jnp.bfloat16).reshape(flat),
        win_dk.astype(jnp.bfloat16).reshape(flat),
        win_dv.astype(jnp.bfloat16).reshape(flat),
    )


def ctx_groups(mesh):
    column = list(mesh.devices[:, 0])
    count = len(column)
    try:
        slow = [tuple(d.coords)[1] for d in column]
    except (AttributeError, TypeError, IndexError):
        return 1, count
    inner = next((i for i, y in enumerate(slow) if y != slow[0]), count)
    if count % inner:
        inner = count
    return count // inner, inner


def solution(mesh):
    outer, inner = ctx_groups(mesh)
    heads = mesh.devices.shape[1]
    split = jax.sharding.Mesh(mesh.devices.reshape(outer, inner, heads), CTX + ("head",))
    spec = P(CTX, "head")
    return jax.shard_map(
        shards,
        mesh=split,
        in_specs=(spec,) * 7,
        out_specs=(spec,) * 7,
        check_vma=False,
    )
```

```python
import math

import jax
import jax.numpy as jnp
from jax import lax
from jax.sharding import PartitionSpec as P

HD = 128
WIN = 512
LANES = 128


PRECISE = lax.Precision.HIGHEST
NORM_EPS = 1e-05


def exclusive_sum(gathered, reverse):
    count = gathered.shape[0]
    index = jnp.arange(count, dtype=jnp.int32)
    if reverse:
        mask = index[None, :] > index[:, None]
    else:
        mask = index[None, :] < index[:, None]
    return jnp.einsum("ij,jf->if", mask.astype(jnp.float32), gathered, precision=PRECISE)


def padded_pieces(vector, count):
    per = -(-vector.shape[0] // count)
    return jnp.pad(vector, (0, per * count - vector.shape[0])).reshape(count, per)


def scan_states(state, outer, inner, reverse, tied=None):
    flat = state.reshape(-1)
    pieces = padded_pieces(flat, lax.axis_size(inner))
    gathered = lax.all_to_all(pieces, inner, 0, 0, tiled=True)
    if tied is not None:
        gathered, tied = lax.optimization_barrier((gathered, tied))
    within = exclusive_sum(gathered, reverse)
    group_total = jnp.sum(gathered, axis=0)
    groups = lax.axis_size(outer)
    copies = jnp.broadcast_to(group_total[None], (groups,) + group_total.shape)
    gathered_totals = lax.all_to_all(copies, outer, 0, 0, tiled=True)
    index = jnp.arange(groups, dtype=jnp.int32)
    mine = lax.axis_index(outer)
    chosen = (index > mine) if reverse else (index < mine)
    across = jnp.einsum(
        "j,jf->f", chosen.astype(jnp.float32), gathered_totals, precision=PRECISE
    )
    returned = lax.all_to_all(within + across[None, :], inner, 0, 0, tiled=True)
    result = returned.reshape(-1)[: flat.shape[0]].reshape(state.shape)
    return result if tied is None else (result, tied)


def head_sum(values, axis):
    count = lax.axis_size(axis)
    copies = jnp.broadcast_to(values[None], (count,) + values.shape)
    return jnp.sum(lax.all_to_all(copies, axis, 0, 0, tiled=True), axis=0)


def passed_along(block, axis, distance):
    devices = range(lax.axis_size(axis[0]) * lax.axis_size(axis[1]))
    route = [(i - distance, i) for i in devices if i - distance in devices]
    return lax.ppermute(block, axis, route)


def causal_rows(block_rows):
    positions = jnp.arange(block_rows, dtype=jnp.int32)
    return positions[:, None] >= positions[None, :]


def linear_forward(query, keys, values, before):
    causal = causal_rows(query.shape[0])
    scores = jnp.einsum("thd,shd->hts", query, keys, preferred_element_type=jnp.float32)
    scores = jnp.where(causal[None], scores, 0.0)
    inner = jnp.einsum("hts,shd->thd", scores, values.astype(jnp.float32), precision=PRECISE)
    result = inner + jnp.einsum(
        "thd,hde->the", query.astype(jnp.float32), before, precision=PRECISE
    )
    return (result, scores)


def linear_backward(query, keys, values, cotangent, scores, before, after):
    causal = causal_rows(query.shape[0])
    cotangent_f = cotangent.astype(jnp.float32)
    dprobs = jnp.einsum("the,she->hts", cotangent, values, preferred_element_type=jnp.float32)
    dprobs = jnp.where(causal[None], dprobs, 0.0)
    query_grad = jnp.einsum("hts,shd->thd", dprobs, keys.astype(jnp.float32), precision=PRECISE)
    query_grad = query_grad + jnp.einsum("the,hde->thd", cotangent_f, before, precision=PRECISE)
    key_grad = jnp.einsum("hts,thd->shd", dprobs, query.astype(jnp.float32), precision=PRECISE)
    key_grad = key_grad + jnp.einsum(
        "she,hde->shd", values.astype(jnp.float32), after, precision=PRECISE
    )
    value_grad = jnp.einsum("hts,the->she", scores, cotangent_f, precision=PRECISE)
    value_grad = value_grad + jnp.einsum(
        "shd,hde->she", keys.astype(jnp.float32), after, precision=PRECISE
    )
    return (query_grad, key_grad, value_grad)


def query_head(query, keys, values, upstream, first_pos):
    row_count = query.shape[0]
    ext_count = keys.shape[0]
    window = ext_count - row_count
    score_scale = 1.0 / math.sqrt(query.shape[2])
    scores = jnp.einsum("thd,shd->hts", query, keys, preferred_element_type=jnp.float32) * score_scale
    query_pos = first_pos + jnp.arange(row_count, dtype=jnp.int32)
    key_pos = first_pos - window + jnp.arange(ext_count, dtype=jnp.int32)
    allowed = (
        (key_pos[None, :] >= 0)
        & (key_pos[None, :] <= query_pos[:, None])
        & (key_pos[None, :] > query_pos[:, None] - window)
    )
    scores = jnp.where(allowed[None], scores, -jnp.inf)
    row_max = jnp.max(scores, axis=2, keepdims=True)
    log_total = row_max[:, :, 0] + jnp.log(jnp.sum(jnp.exp(scores - row_max), axis=2))
    probs = jnp.exp(scores - log_total[:, :, None])
    weights_low = probs.astype(jnp.bfloat16)
    output = jnp.einsum("hts,shd->thd", weights_low, values, preferred_element_type=jnp.float32)
    dprobs = jnp.einsum("thd,shd->hts", upstream, values, preferred_element_type=jnp.float32)
    row_dot = jnp.sum(probs * dprobs, axis=2)
    dscores = (probs * (dprobs - row_dot[:, :, None]) * score_scale).astype(jnp.bfloat16)
    query_grad = jnp.einsum("hts,shd->thd", dscores, keys, preferred_element_type=jnp.float32)
    return (output, query_grad, log_total, row_dot)


def key_head(query, upstream, totals, dots, keys, values, first_pos, total_rows):
    row_count = keys.shape[0]
    ext_count = query.shape[0]
    window = ext_count - row_count
    score_scale = 1.0 / math.sqrt(query.shape[2])
    scores = jnp.einsum("thd,shd->hts", query, keys, preferred_element_type=jnp.float32) * score_scale
    query_pos = first_pos + jnp.arange(ext_count, dtype=jnp.int32)
    key_pos = first_pos + jnp.arange(row_count, dtype=jnp.int32)
    allowed = (
        (query_pos[:, None] < total_rows)
        & (key_pos[None, :] <= query_pos[:, None])
        & (key_pos[None, :] > query_pos[:, None] - window)
    )
    probs = jnp.where(allowed[None], jnp.exp(scores - totals[:, :, None]), 0.0)
    weights_low = probs.astype(jnp.bfloat16)
    dprobs = jnp.einsum("thd,shd->hts", upstream, values, preferred_element_type=jnp.float32)
    dscores = (probs * (dprobs - dots[:, :, None]) * score_scale).astype(jnp.bfloat16)
    key_grad = jnp.einsum("hts,thd->shd", dscores, query, preferred_element_type=jnp.float32)
    value_grad = jnp.einsum("hts,thd->shd", weights_low, upstream, preferred_element_type=jnp.float32)
    return (key_grad, value_grad)


CTX = ("cy", "cz")


def shards(lin_q, lin_k, lin_v, win_q, win_k, win_v, grad_out):
    row_count = lin_q.shape[0]
    head_count = lin_q.shape[1] // HD
    shaped = (row_count, head_count, HD)
    flat = (row_count, head_count * HD)
    span = WIN // row_count
    total_rows = row_count * lax.axis_size(CTX[0]) * lax.axis_size(CTX[1])
    first_pos = lax.axis_index(CTX) * row_count
    win_query = win_q.reshape(shaped)
    win_key = win_k.reshape(shaped)
    win_value = win_v.reshape(shaped)
    cotangent = grad_out.reshape(shaped)

    earlier_keys, earlier_values = [], []
    later_queries, later_upstreams = [], []
    own_keys = jnp.stack([win_key, win_value])
    own_rows = jnp.stack([win_query, cotangent])
    for distance in range(1, span + 1):
        key_pair = passed_along(own_keys, CTX, distance)
        row_pair = passed_along(own_rows, CTX, -distance)
        earlier_keys.insert(0, key_pair[0])
        earlier_values.insert(0, key_pair[1])
        later_queries.append(row_pair[0])
        later_upstreams.append(row_pair[1])

    lin_query = lin_q.reshape(shaped)
    lin_key = lin_k.reshape(shaped)
    lin_value = lin_v.reshape(shaped)
    key_state = jnp.einsum("shd,she->hde", lin_key, lin_value, preferred_element_type=jnp.float32)
    prefix = scan_states(key_state, CTX[0], CTX[1], False)
    lin_out, lin_scores = linear_forward(lin_query, lin_key, lin_value, prefix)
    upstream = grad_out.reshape(shaped).astype(jnp.float32)
    square_sum, cross_sum = head_sum(
        jnp.stack([jnp.sum(lin_out * lin_out, axis=(1, 2)), jnp.sum(upstream * lin_out, axis=(1, 2))]),
        "head",
    )
    features = head_count * HD * lax.axis_size("head")
    inv_rms = lax.rsqrt(square_sum / features + NORM_EPS)
    lin_dout = (
        inv_rms[:, None, None] * upstream
        - lin_out * (inv_rms**3 * cross_sum / features)[:, None, None]
    ).astype(jnp.bfloat16)
    query_state = jnp.einsum(
        "thd,the->hde", lin_query, lin_dout, preferred_element_type=jnp.float32
    )
    key_ext = jnp.concatenate(earlier_keys + [win_key], axis=0)
    value_ext = jnp.concatenate(earlier_values + [win_value], axis=0)
    win_out, win_dq, log_total, row_dot = query_head(
        win_query, key_ext, value_ext, cotangent, first_pos
    )

    suffix, own_stats = scan_states(
        query_state, CTX[0], CTX[1], True, tied=jnp.stack([log_total, row_dot])
    )
    grad_q, grad_k, grad_v = linear_backward(
        lin_query, lin_key, lin_value, lin_dout, lin_scores, prefix, suffix
    )

    later_totals, later_dots = [], []
    for distance in range(1, span + 1):
        stat_pair = passed_along(own_stats, CTX, -distance)
        later_totals.append(stat_pair[0])
        later_dots.append(stat_pair[1])
    query_ext = jnp.concatenate([win_query] + later_queries, axis=0)
    upstream_ext = jnp.concatenate([cotangent] + later_upstreams, axis=0)
    total_ext = jnp.concatenate([log_total] + later_totals, axis=1)
    dot_ext = jnp.concatenate([row_dot] + later_dots, axis=1)
    win_dk, win_dv = key_head(
        query_ext, upstream_ext, total_ext, dot_ext, win_key, win_value, first_pos, total_rows
    )
    mixed = (lin_out * inv_rms[:, None, None] + win_out).astype(jnp.bfloat16).reshape(flat)
    return (
        mixed,
        grad_q.astype(jnp.bfloat16).reshape(flat),
        grad_k.astype(jnp.bfloat16).reshape(flat),
        grad_v.astype(jnp.bfloat16).reshape(flat),
        win_dq.astype(jnp.bfloat16).reshape(flat),
        win_dk.astype(jnp.bfloat16).reshape(flat),
        win_dv.astype(jnp.bfloat16).reshape(flat),
    )


def ctx_groups(mesh):
    column = list(mesh.devices[:, 0])
    count = len(column)
    try:
        slow = [tuple(d.coords)[1] for d in column]
    except (AttributeError, TypeError, IndexError):
        return 1, count
    inner = next((i for i, y in enumerate(slow) if y != slow[0]), count)
    if count % inner:
        inner = count
    return count // inner, inner


def solution(mesh):
    outer, inner = ctx_groups(mesh)
    heads = mesh.devices.shape[1]
    split = jax.sharding.Mesh(mesh.devices.reshape(outer, inner, heads), CTX + ("head",))
    spec = P(CTX, "head")
    return jax.shard_map(
        shards,
        mesh=split,
        in_specs=(spec,) * 7,
        out_specs=(spec,) * 7,
        check_vma=False,
    )
```

```python
import math

import jax
import jax.numpy as jnp
from jax import lax
from jax.sharding import PartitionSpec as P

HD = 128
WIN = 512
LANES = 128


PRECISE = lax.Precision.HIGHEST
NORM_EPS = 1e-05


def exclusive_sum(gathered, reverse):
    count = gathered.shape[0]
    index = jnp.arange(count, dtype=jnp.int32)
    if reverse:
        mask = index[None, :] > index[:, None]
    else:
        mask = index[None, :] < index[:, None]
    return jnp.einsum("ij,jf->if", mask.astype(jnp.float32), gathered, precision=PRECISE)


def padded_pieces(vector, count):
    per = -(-vector.shape[0] // count)
    return jnp.pad(vector, (0, per * count - vector.shape[0])).reshape(count, per)


def scan_states(state, outer, inner, reverse, tied=None):
    flat = state.reshape(-1)
    pieces = padded_pieces(flat, lax.axis_size(inner))
    gathered = lax.all_to_all(pieces, inner, 0, 0, tiled=True)
    if tied is not None:
        gathered, tied = lax.optimization_barrier((gathered, tied))
    within = exclusive_sum(gathered, reverse)
    group_total = jnp.sum(gathered, axis=0)
    groups = lax.axis_size(outer)
    copies = jnp.broadcast_to(group_total[None], (groups,) + group_total.shape)
    gathered_totals = lax.all_to_all(copies, outer, 0, 0, tiled=True)
    index = jnp.arange(groups, dtype=jnp.int32)
    mine = lax.axis_index(outer)
    chosen = (index > mine) if reverse else (index < mine)
    across = jnp.einsum(
        "j,jf->f", chosen.astype(jnp.float32), gathered_totals, precision=PRECISE
    )
    returned = lax.all_to_all(within + across[None, :], inner, 0, 0, tiled=True)
    result = returned.reshape(-1)[: flat.shape[0]].reshape(state.shape)
    return result if tied is None else (result, tied)


def head_sum(values, axis):
    count = lax.axis_size(axis)
    copies = jnp.broadcast_to(values[None], (count,) + values.shape)
    return jnp.sum(lax.all_to_all(copies, axis, 0, 0, tiled=True), axis=0)


def passed_along(block, axis, distance):
    devices = range(lax.axis_size(axis[0]) * lax.axis_size(axis[1]))
    route = [(i - distance, i) for i in devices if i - distance in devices]
    return lax.ppermute(block, axis, route)


def causal_rows(block_rows):
    positions = jnp.arange(block_rows, dtype=jnp.int32)
    return positions[:, None] >= positions[None, :]


def linear_forward(query, keys, values, before):
    causal = causal_rows(query.shape[0])
    scores = jnp.einsum("thd,shd->hts", query, keys, preferred_element_type=jnp.float32)
    scores = jnp.where(causal[None], scores, 0.0)
    inner = jnp.einsum("hts,shd->thd", scores, values.astype(jnp.float32), precision=PRECISE)
    result = inner + jnp.einsum(
        "thd,hde->the", query.astype(jnp.float32), before, precision=PRECISE
    )
    return (result, scores)


def linear_backward(query, keys, values, cotangent, scores, before, after):
    causal = causal_rows(query.shape[0])
    cotangent_f = cotangent.astype(jnp.float32)
    dprobs = jnp.einsum("the,she->hts", cotangent, values, preferred_element_type=jnp.float32)
    dprobs = jnp.where(causal[None], dprobs, 0.0)
    query_grad = jnp.einsum("hts,shd->thd", dprobs, keys.astype(jnp.float32), precision=PRECISE)
    query_grad = query_grad + jnp.einsum("the,hde->thd", cotangent_f, before, precision=PRECISE)
    key_grad = jnp.einsum("hts,thd->shd", dprobs, query.astype(jnp.float32), precision=PRECISE)
    key_grad = key_grad + jnp.einsum(
        "she,hde->shd", values.astype(jnp.float32), after, precision=PRECISE
    )
    value_grad = jnp.einsum("hts,the->she", scores, cotangent_f, precision=PRECISE)
    value_grad = value_grad + jnp.einsum(
        "shd,hde->she", keys.astype(jnp.float32), after, precision=PRECISE
    )
    return (query_grad, key_grad, value_grad)


def query_head(query, keys, values, upstream, first_pos):
    row_count = query.shape[0]
    ext_count = keys.shape[0]
    window = ext_count - row_count
    score_scale = 1.0 / math.sqrt(query.shape[2])
    scores = jnp.einsum("thd,shd->hts", query, keys, preferred_element_type=jnp.float32) * score_scale
    query_pos = first_pos + jnp.arange(row_count, dtype=jnp.int32)
    key_pos = first_pos - window + jnp.arange(ext_count, dtype=jnp.int32)
    allowed = (
        (key_pos[None, :] >= 0)
        & (key_pos[None, :] <= query_pos[:, None])
        & (key_pos[None, :] > query_pos[:, None] - window)
    )
    scores = jnp.where(allowed[None], scores, -jnp.inf)
    row_max = jnp.max(scores, axis=2, keepdims=True)
    log_total = row_max[:, :, 0] + jnp.log(jnp.sum(jnp.exp(scores - row_max), axis=2))
    probs = jnp.exp(scores - log_total[:, :, None])
    weights_low = probs.astype(jnp.bfloat16)
    output = jnp.einsum("hts,shd->thd", weights_low, values, preferred_element_type=jnp.float32)
    dprobs = jnp.einsum("thd,shd->hts", upstream, values, preferred_element_type=jnp.float32)
    row_dot = jnp.sum(probs * dprobs, axis=2)
    dscores = (probs * (dprobs - row_dot[:, :, None]) * score_scale).astype(jnp.bfloat16)
    query_grad = jnp.einsum("hts,shd->thd", dscores, keys, preferred_element_type=jnp.float32)
    return (output, query_grad, log_total, row_dot)


def key_head(query, upstream, totals, dots, keys, values, first_pos, total_rows):
    row_count = keys.shape[0]
    ext_count = query.shape[0]
    window = ext_count - row_count
    score_scale = 1.0 / math.sqrt(query.shape[2])
    scores = jnp.einsum("thd,shd->hts", query, keys, preferred_element_type=jnp.float32) * score_scale
    query_pos = first_pos + jnp.arange(ext_count, dtype=jnp.int32)
    key_pos = first_pos + jnp.arange(row_count, dtype=jnp.int32)
    allowed = (
        (query_pos[:, None] < total_rows)
        & (key_pos[None, :] <= query_pos[:, None])
        & (key_pos[None, :] > query_pos[:, None] - window)
    )
    probs = jnp.where(allowed[None], jnp.exp(scores - totals[:, :, None]), 0.0)
    weights_low = probs.astype(jnp.bfloat16)
    dprobs = jnp.einsum("thd,shd->hts", upstream, values, preferred_element_type=jnp.float32)
    dscores = (probs * (dprobs - dots[:, :, None]) * score_scale).astype(jnp.bfloat16)
    key_grad = jnp.einsum("hts,thd->shd", dscores, query, preferred_element_type=jnp.float32)
    value_grad = jnp.einsum("hts,thd->shd", weights_low, upstream, preferred_element_type=jnp.float32)
    return (key_grad, value_grad)


CTX = ("cy", "cz")


def shards(lin_q, lin_k, lin_v, win_q, win_k, win_v, grad_out):
    row_count = lin_q.shape[0]
    head_count = lin_q.shape[1] // HD
    shaped = (row_count, head_count, HD)
    flat = (row_count, head_count * HD)
    span = WIN // row_count
    total_rows = row_count * lax.axis_size(CTX[0]) * lax.axis_size(CTX[1])
    first_pos = lax.axis_index(CTX) * row_count
    win_query = win_q.reshape(shaped)
    win_key = win_k.reshape(shaped)
    win_value = win_v.reshape(shaped)
    cotangent = grad_out.reshape(shaped)

    earlier_keys, earlier_values = [], []
    later_queries, later_upstreams = [], []
    key_pair = jnp.stack([win_key, win_value])
    row_pair = jnp.stack([win_query, cotangent])
    for _ in range(span):
        key_pair = passed_along(key_pair, CTX, 1)
        row_pair = passed_along(row_pair, CTX, -1)
        earlier_keys.insert(0, key_pair[0])
        earlier_values.insert(0, key_pair[1])
        later_queries.append(row_pair[0])
        later_upstreams.append(row_pair[1])

    lin_query = lin_q.reshape(shaped)
    lin_key = lin_k.reshape(shaped)
    lin_value = lin_v.reshape(shaped)
    key_state = jnp.einsum("shd,she->hde", lin_key, lin_value, preferred_element_type=jnp.float32)
    prefix = scan_states(key_state, CTX[0], CTX[1], False)
    lin_out, lin_scores = linear_forward(lin_query, lin_key, lin_value, prefix)
    upstream = grad_out.reshape(shaped).astype(jnp.float32)
    square_sum, cross_sum = head_sum(
        jnp.stack([jnp.sum(lin_out * lin_out, axis=(1, 2)), jnp.sum(upstream * lin_out, axis=(1, 2))]),
        "head",
    )
    features = head_count * HD * lax.axis_size("head")
    inv_rms = lax.rsqrt(square_sum / features + NORM_EPS)
    lin_dout = (
        inv_rms[:, None, None] * upstream
        - lin_out * (inv_rms**3 * cross_sum / features)[:, None, None]
    ).astype(jnp.bfloat16)
    query_state = jnp.einsum(
        "thd,the->hde", lin_query, lin_dout, preferred_element_type=jnp.float32
    )
    key_ext = jnp.concatenate(earlier_keys + [win_key], axis=0)
    value_ext = jnp.concatenate(earlier_values + [win_value], axis=0)
    win_out, win_dq, log_total, row_dot = query_head(
        win_query, key_ext, value_ext, cotangent, first_pos
    )

    suffix, own_stats = scan_states(
        query_state, CTX[0], CTX[1], True, tied=jnp.stack([log_total, row_dot])
    )
    grad_q, grad_k, grad_v = linear_backward(
        lin_query, lin_key, lin_value, lin_dout, lin_scores, prefix, suffix
    )

    later_totals, later_dots = [], []
    for distance in range(1, span + 1):
        stat_pair = passed_along(own_stats, CTX, -distance)
        later_totals.append(stat_pair[0])
        later_dots.append(stat_pair[1])
    query_ext = jnp.concatenate([win_query] + later_queries, axis=0)
    upstream_ext = jnp.concatenate([cotangent] + later_upstreams, axis=0)
    total_ext = jnp.concatenate([log_total] + later_totals, axis=1)
    dot_ext = jnp.concatenate([row_dot] + later_dots, axis=1)
    win_dk, win_dv = key_head(
        query_ext, upstream_ext, total_ext, dot_ext, win_key, win_value, first_pos, total_rows
    )
    mixed = (lin_out * inv_rms[:, None, None] + win_out).astype(jnp.bfloat16).reshape(flat)
    return (
        mixed,
        grad_q.astype(jnp.bfloat16).reshape(flat),
        grad_k.astype(jnp.bfloat16).reshape(flat),
        grad_v.astype(jnp.bfloat16).reshape(flat),
        win_dq.astype(jnp.bfloat16).reshape(flat),
        win_dk.astype(jnp.bfloat16).reshape(flat),
        win_dv.astype(jnp.bfloat16).reshape(flat),
    )


def ctx_groups(mesh):
    column = list(mesh.devices[:, 0])
    count = len(column)
    try:
        slow = [tuple(d.coords)[1] for d in column]
    except (AttributeError, TypeError, IndexError):
        return 1, count
    inner = next((i for i, y in enumerate(slow) if y != slow[0]), count)
    if count % inner:
        inner = count
    return count // inner, inner


def solution(mesh):
    outer, inner = ctx_groups(mesh)
    heads = mesh.devices.shape[1]
    split = jax.sharding.Mesh(mesh.devices.reshape(outer, inner, heads), CTX + ("head",))
    spec = P(CTX, "head")
    return jax.shard_map(
        shards,
        mesh=split,
        in_specs=(spec,) * 7,
        out_specs=(spec,) * 7,
        check_vma=False,
    )
```

```python
import math
from functools import partial

import jax
import jax.numpy as jnp
from jax import lax
from jax.experimental import pallas as pl
from jax.experimental.pallas import tpu as pltpu
from jax.sharding import PartitionSpec as P

HD = 128
WIN = 512
LANES = 128


PRECISE = lax.Precision.HIGHEST
NORM_EPS = 1e-05
INTERPRET = False


def exclusive_sum(gathered, reverse):
    count = gathered.shape[0]
    index = jnp.arange(count, dtype=jnp.int32)
    if reverse:
        mask = index[None, :] > index[:, None]
    else:
        mask = index[None, :] < index[:, None]
    return jnp.einsum("ij,jf->if", mask.astype(jnp.float32), gathered, precision=PRECISE)


def padded_pieces(vector, count):
    per = -(-vector.shape[0] // count)
    return jnp.pad(vector, (0, per * count - vector.shape[0])).reshape(count, per)


def scan_states(state, outer, inner, reverse):
    flat = state.reshape(-1)
    pieces = padded_pieces(flat, lax.axis_size(inner))
    gathered = lax.all_to_all(pieces, inner, 0, 0, tiled=True)
    within = exclusive_sum(gathered, reverse)
    group_total = jnp.sum(gathered, axis=0)
    groups = lax.axis_size(outer)
    copies = jnp.broadcast_to(group_total[None], (groups,) + group_total.shape)
    gathered_totals = lax.all_to_all(copies, outer, 0, 0, tiled=True)
    index = jnp.arange(groups, dtype=jnp.int32)
    mine = lax.axis_index(outer)
    chosen = (index > mine) if reverse else (index < mine)
    across = jnp.einsum(
        "j,jf->f", chosen.astype(jnp.float32), gathered_totals, precision=PRECISE
    )
    returned = lax.all_to_all(within + across[None, :], inner, 0, 0, tiled=True)
    return returned.reshape(-1)[: flat.shape[0]].reshape(state.shape)


def head_sum(values, axis):
    count = lax.axis_size(axis)
    copies = jnp.broadcast_to(values[None], (count,) + values.shape)
    return jnp.sum(lax.all_to_all(copies, axis, 0, 0, tiled=True), axis=0)


def passed_along(block, axis, distance):
    devices = range(lax.axis_size(axis[0]) * lax.axis_size(axis[1]))
    route = [(i - distance, i) for i in devices if i - distance in devices]
    return lax.ppermute(block, axis, route)


def causal_rows(block_rows):
    positions = jnp.arange(block_rows, dtype=jnp.int32)
    return positions[:, None] >= positions[None, :]


def linear_forward(query, keys, values, before):
    causal = causal_rows(query.shape[0])
    scores = jnp.einsum("thd,shd->hts", query, keys, preferred_element_type=jnp.float32)
    scores = jnp.where(causal[None], scores, 0.0)
    inner = jnp.einsum("hts,shd->thd", scores, values.astype(jnp.float32), precision=PRECISE)
    result = inner + jnp.einsum(
        "thd,hde->the", query.astype(jnp.float32), before, precision=PRECISE
    )
    return (result, scores)


def linear_backward(query, keys, values, cotangent, scores, before, after):
    causal = causal_rows(query.shape[0])
    cotangent_f = cotangent.astype(jnp.float32)
    dprobs = jnp.einsum("the,she->hts", cotangent, values, preferred_element_type=jnp.float32)
    dprobs = jnp.where(causal[None], dprobs, 0.0)
    query_grad = jnp.einsum("hts,shd->thd", dprobs, keys.astype(jnp.float32), precision=PRECISE)
    query_grad = query_grad + jnp.einsum("the,hde->thd", cotangent_f, before, precision=PRECISE)
    key_grad = jnp.einsum("hts,thd->shd", dprobs, query.astype(jnp.float32), precision=PRECISE)
    key_grad = key_grad + jnp.einsum(
        "she,hde->shd", values.astype(jnp.float32), after, precision=PRECISE
    )
    value_grad = jnp.einsum("hts,the->she", scores, cotangent_f, precision=PRECISE)
    value_grad = value_grad + jnp.einsum(
        "shd,hde->she", keys.astype(jnp.float32), after, precision=PRECISE
    )
    return (query_grad, key_grad, value_grad)


def query_head(query, keys, values, upstream, first_pos):
    row_count = query.shape[0]
    ext_count = keys.shape[0]
    window = ext_count - row_count
    score_scale = 1.0 / math.sqrt(query.shape[2])
    scores = jnp.einsum("thd,shd->hts", query, keys, preferred_element_type=jnp.float32) * score_scale
    query_pos = first_pos + jnp.arange(row_count, dtype=jnp.int32)
    key_pos = first_pos - window + jnp.arange(ext_count, dtype=jnp.int32)
    allowed = (
        (key_pos[None, :] >= 0)
        & (key_pos[None, :] <= query_pos[:, None])
        & (key_pos[None, :] > query_pos[:, None] - window)
    )
    scores = jnp.where(allowed[None], scores, -jnp.inf)
    row_max = jnp.max(scores, axis=2, keepdims=True)
    log_total = row_max[:, :, 0] + jnp.log(jnp.sum(jnp.exp(scores - row_max), axis=2))
    probs = jnp.exp(scores - log_total[:, :, None])
    weights_low = probs.astype(jnp.bfloat16)
    output = jnp.einsum("hts,shd->thd", weights_low, values, preferred_element_type=jnp.float32)
    dprobs = jnp.einsum("thd,shd->hts", upstream, values, preferred_element_type=jnp.float32)
    row_dot = jnp.sum(probs * dprobs, axis=2)
    dscores = (probs * (dprobs - row_dot[:, :, None]) * score_scale).astype(jnp.bfloat16)
    query_grad = jnp.einsum("hts,shd->thd", dscores, keys, preferred_element_type=jnp.float32)
    return (output, query_grad, log_total, row_dot)


def key_head(query, upstream, totals, dots, keys, values, first_pos, total_rows):
    row_count = keys.shape[0]
    ext_count = query.shape[0]
    window = ext_count - row_count
    score_scale = 1.0 / math.sqrt(query.shape[2])
    scores = jnp.einsum("thd,shd->hts", query, keys, preferred_element_type=jnp.float32) * score_scale
    query_pos = first_pos + jnp.arange(ext_count, dtype=jnp.int32)
    key_pos = first_pos + jnp.arange(row_count, dtype=jnp.int32)
    allowed = (
        (query_pos[:, None] < total_rows)
        & (key_pos[None, :] <= query_pos[:, None])
        & (key_pos[None, :] > query_pos[:, None] - window)
    )
    probs = jnp.where(allowed[None], jnp.exp(scores - totals[:, :, None]), 0.0)
    weights_low = probs.astype(jnp.bfloat16)
    dprobs = jnp.einsum("thd,shd->hts", upstream, values, preferred_element_type=jnp.float32)
    dscores = (probs * (dprobs - dots[:, :, None]) * score_scale).astype(jnp.bfloat16)
    key_grad = jnp.einsum("hts,thd->shd", dscores, query, preferred_element_type=jnp.float32)
    value_grad = jnp.einsum("hts,thd->shd", weights_low, upstream, preferred_element_type=jnp.float32)
    return (key_grad, value_grad)


def key_side_kernel(pos_ref, query_ref, upstream_ref, totals_ref, dots_ref, keys_ref, values_ref,
                    key_grad_ref, value_grad_ref, *, window, total_rows, score_scale):
    first_pos = pos_ref[0]
    query = query_ref[...]
    upstream = upstream_ref[...]
    keys = keys_ref[...]
    values = values_ref[...]
    contract_last = (((1,), (1,)), ((), ()))
    scores = lax.dot_general(keys, query, contract_last, preferred_element_type=jnp.float32) * score_scale
    row_count, ext_count = scores.shape
    key_pos = first_pos + lax.broadcasted_iota(jnp.int32, (row_count, ext_count), 0)
    query_pos = first_pos + lax.broadcasted_iota(jnp.int32, (row_count, ext_count), 1)
    allowed = (query_pos < total_rows) & (key_pos <= query_pos) & (key_pos > query_pos - window)
    probs = jnp.where(allowed, jnp.exp(scores - totals_ref[0]), 0.0)
    weights_low = probs.astype(jnp.bfloat16)
    dprobs = lax.dot_general(values, upstream, contract_last, preferred_element_type=jnp.float32)
    dscores = (probs * (dprobs - dots_ref[0]) * score_scale).astype(jnp.bfloat16)
    key_grad_ref[...] = jnp.dot(dscores, query, preferred_element_type=jnp.float32)
    value_grad_ref[...] = jnp.dot(weights_low, upstream, preferred_element_type=jnp.float32)


def key_side(query, upstream, totals, dots, keys, values, first_pos, total_rows):
    ext_count = query.shape[0]
    row_count = keys.shape[0]
    head_count = keys.shape[1] // HD
    body = partial(
        key_side_kernel,
        window=ext_count - row_count,
        total_rows=total_rows,
        score_scale=1.0 / math.sqrt(HD),
    )
    ext_spec = pl.BlockSpec((ext_count, HD), lambda h, pos: (0, h))
    stat_spec = pl.BlockSpec((1, 1, ext_count), lambda h, pos: (h, 0, 0))
    row_spec = pl.BlockSpec((row_count, HD), lambda h, pos: (0, h))
    grad = jax.ShapeDtypeStruct(keys.shape, jnp.float32)
    return pl.pallas_call(
        body,
        grid_spec=pltpu.PrefetchScalarGridSpec(
            num_scalar_prefetch=1,
            grid=(head_count,),
            in_specs=[ext_spec, ext_spec, stat_spec, stat_spec, row_spec, row_spec],
            out_specs=[row_spec, row_spec],
        ),
        out_shape=[grad, grad],
        interpret=INTERPRET,
    )(
        jnp.reshape(first_pos, (1,)).astype(jnp.int32),
        query,
        upstream,
        totals.reshape(head_count, 1, ext_count),
        dots.reshape(head_count, 1, ext_count),
        keys,
        values,
    )


CTX = ("cy", "cz")


def shards(lin_q, lin_k, lin_v, win_q, win_k, win_v, grad_out):
    row_count = lin_q.shape[0]
    head_count = lin_q.shape[1] // HD
    shaped = (row_count, head_count, HD)
    flat = (row_count, head_count * HD)
    span = WIN // row_count
    total_rows = row_count * lax.axis_size(CTX[0]) * lax.axis_size(CTX[1])
    first_pos = lax.axis_index(CTX) * row_count
    win_query = win_q.reshape(shaped)
    win_key = win_k.reshape(shaped)
    win_value = win_v.reshape(shaped)
    cotangent = grad_out.reshape(shaped)

    earlier_keys, earlier_values = [], []
    later_queries, later_upstreams = [], []
    key_pair = jnp.stack([win_key, win_value])
    row_pair = jnp.stack([win_query, cotangent])
    for _ in range(span):
        key_pair = passed_along(key_pair, CTX, 1)
        row_pair = passed_along(row_pair, CTX, -1)
        earlier_keys.insert(0, key_pair[0])
        earlier_values.insert(0, key_pair[1])
        later_queries.append(row_pair[0])
        later_upstreams.append(row_pair[1])

    lin_query = lin_q.reshape(shaped)
    lin_key = lin_k.reshape(shaped)
    lin_value = lin_v.reshape(shaped)
    key_state = jnp.einsum("shd,she->hde", lin_key, lin_value, preferred_element_type=jnp.float32)
    prefix = scan_states(key_state, CTX[0], CTX[1], False)
    lin_out, lin_scores = linear_forward(lin_query, lin_key, lin_value, prefix)
    upstream = grad_out.reshape(shaped).astype(jnp.float32)
    square_sum, cross_sum = head_sum(
        jnp.stack([jnp.sum(lin_out * lin_out, axis=(1, 2)), jnp.sum(upstream * lin_out, axis=(1, 2))]),
        "head",
    )
    features = head_count * HD * lax.axis_size("head")
    inv_rms = lax.rsqrt(square_sum / features + NORM_EPS)
    lin_dout = (
        inv_rms[:, None, None] * upstream
        - lin_out * (inv_rms**3 * cross_sum / features)[:, None, None]
    ).astype(jnp.bfloat16)
    query_state = jnp.einsum(
        "thd,the->hde", lin_query, lin_dout, preferred_element_type=jnp.float32
    )
    suffix = scan_states(query_state, CTX[0], CTX[1], True)
    grad_q, grad_k, grad_v = linear_backward(
        lin_query, lin_key, lin_value, lin_dout, lin_scores, prefix, suffix
    )

    key_ext = jnp.concatenate(earlier_keys + [win_key], axis=0)
    value_ext = jnp.concatenate(earlier_values + [win_value], axis=0)
    win_out, win_dq, log_total, row_dot = query_head(
        win_query, key_ext, value_ext, cotangent, first_pos
    )

    later_totals, later_dots = [], []
    stat_pair = jnp.stack([log_total, row_dot])
    for distance in range(1, span + 1):
        stat_pair = passed_along(jnp.stack([log_total, row_dot]), CTX, -distance)
        later_totals.append(stat_pair[0])
        later_dots.append(stat_pair[1])
    query_ext = jnp.concatenate([win_query] + later_queries, axis=0)
    upstream_ext = jnp.concatenate([cotangent] + later_upstreams, axis=0)
    total_ext = jnp.concatenate([log_total] + later_totals, axis=1)
    dot_ext = jnp.concatenate([row_dot] + later_dots, axis=1)
    win_dk, win_dv = key_side(
        query_ext.reshape(-1, head_count * HD),
        upstream_ext.reshape(-1, head_count * HD),
        total_ext,
        dot_ext,
        win_k,
        win_v,
        first_pos,
        total_rows,
    )
    mixed = (lin_out * inv_rms[:, None, None] + win_out).astype(jnp.bfloat16).reshape(flat)
    return (
        mixed,
        grad_q.astype(jnp.bfloat16).reshape(flat),
        grad_k.astype(jnp.bfloat16).reshape(flat),
        grad_v.astype(jnp.bfloat16).reshape(flat),
        win_dq.astype(jnp.bfloat16).reshape(flat),
        win_dk.astype(jnp.bfloat16),
        win_dv.astype(jnp.bfloat16),
    )


def ctx_groups(mesh):
    column = list(mesh.devices[:, 0])
    count = len(column)
    try:
        slow = [tuple(d.coords)[1] for d in column]
    except (AttributeError, TypeError, IndexError):
        return 1, count
    inner = next((i for i, y in enumerate(slow) if y != slow[0]), count)
    if count % inner:
        inner = count
    return count // inner, inner


def solution(mesh):
    outer, inner = ctx_groups(mesh)
    heads = mesh.devices.shape[1]
    split = jax.sharding.Mesh(mesh.devices.reshape(outer, inner, heads), CTX + ("head",))
    spec = P(CTX, "head")
    return jax.shard_map(
        shards,
        mesh=split,
        in_specs=(spec,) * 7,
        out_specs=(spec,) * 7,
        check_vma=False,
    )
```

```python
import math

import jax
import jax.numpy as jnp
from jax import lax
from jax.sharding import PartitionSpec as P

HD = 128
WIN = 512
LANES = 128


PRECISE = lax.Precision.HIGHEST
NORM_EPS = 1e-05


def exclusive_sum(gathered, reverse):
    count = gathered.shape[0]
    index = jnp.arange(count, dtype=jnp.int32)
    if reverse:
        mask = index[None, :] > index[:, None]
    else:
        mask = index[None, :] < index[:, None]
    return jnp.einsum("ij,jf->if", mask.astype(jnp.float32), gathered, precision=PRECISE)


def padded_pieces(vector, count):
    per = -(-vector.shape[0] // count)
    return jnp.pad(vector, (0, per * count - vector.shape[0])).reshape(count, per)


def scan_states(state, outer, inner, reverse):
    flat = state.reshape(-1)
    pieces = padded_pieces(flat, lax.axis_size(inner))
    gathered = lax.all_to_all(pieces, inner, 0, 0, tiled=True)
    within = exclusive_sum(gathered, reverse)
    group_total = jnp.sum(gathered, axis=0)
    groups = lax.axis_size(outer)
    copies = jnp.broadcast_to(group_total[None], (groups,) + group_total.shape)
    gathered_totals = lax.all_to_all(copies, outer, 0, 0, tiled=True)
    index = jnp.arange(groups, dtype=jnp.int32)
    mine = lax.axis_index(outer)
    chosen = (index > mine) if reverse else (index < mine)
    across = jnp.einsum(
        "j,jf->f", chosen.astype(jnp.float32), gathered_totals, precision=PRECISE
    )
    returned = lax.all_to_all(within + across[None, :], inner, 0, 0, tiled=True)
    return returned.reshape(-1)[: flat.shape[0]].reshape(state.shape)


def scan_flat(state, axis, reverse):
    flat = state.reshape(-1)
    pieces = padded_pieces(flat, lax.axis_size(axis[0]) * lax.axis_size(axis[1]))
    gathered = lax.all_to_all(pieces, axis, 0, 0, tiled=True)
    returned = lax.all_to_all(exclusive_sum(gathered, reverse), axis, 0, 0, tiled=True)
    return returned.reshape(-1)[: flat.shape[0]].reshape(state.shape)


def head_sum(values, axis):
    count = lax.axis_size(axis)
    copies = jnp.broadcast_to(values[None], (count,) + values.shape)
    return jnp.sum(lax.all_to_all(copies, axis, 0, 0, tiled=True), axis=0)


def passed_along(block, axis, distance):
    devices = range(lax.axis_size(axis[0]) * lax.axis_size(axis[1]))
    route = [(i - distance, i) for i in devices if i - distance in devices]
    return lax.ppermute(block, axis, route)


def causal_rows(block_rows):
    positions = jnp.arange(block_rows, dtype=jnp.int32)
    return positions[:, None] >= positions[None, :]


def linear_forward(query, keys, values, before):
    causal = causal_rows(query.shape[0])
    scores = jnp.einsum("thd,shd->hts", query, keys, preferred_element_type=jnp.float32)
    scores = jnp.where(causal[None], scores, 0.0)
    inner = jnp.einsum("hts,shd->thd", scores, values.astype(jnp.float32), precision=PRECISE)
    result = inner + jnp.einsum(
        "thd,hde->the", query.astype(jnp.float32), before, precision=PRECISE
    )
    return (result, scores)


def linear_backward(query, keys, values, cotangent, scores, before, after):
    causal = causal_rows(query.shape[0])
    cotangent_f = cotangent.astype(jnp.float32)
    dprobs = jnp.einsum("the,she->hts", cotangent, values, preferred_element_type=jnp.float32)
    dprobs = jnp.where(causal[None], dprobs, 0.0)
    query_grad = jnp.einsum("hts,shd->thd", dprobs, keys.astype(jnp.float32), precision=PRECISE)
    query_grad = query_grad + jnp.einsum("the,hde->thd", cotangent_f, before, precision=PRECISE)
    key_grad = jnp.einsum("hts,thd->shd", dprobs, query.astype(jnp.float32), precision=PRECISE)
    key_grad = key_grad + jnp.einsum(
        "she,hde->shd", values.astype(jnp.float32), after, precision=PRECISE
    )
    value_grad = jnp.einsum("hts,the->she", scores, cotangent_f, precision=PRECISE)
    value_grad = value_grad + jnp.einsum(
        "shd,hde->she", keys.astype(jnp.float32), after, precision=PRECISE
    )
    return (query_grad, key_grad, value_grad)


def query_head(query, keys, values, upstream, first_pos):
    row_count = query.shape[0]
    ext_count = keys.shape[0]
    window = ext_count - row_count
    score_scale = 1.0 / math.sqrt(query.shape[2])
    scores = jnp.einsum("thd,shd->hts", query, keys, preferred_element_type=jnp.float32) * score_scale
    query_pos = first_pos + jnp.arange(row_count, dtype=jnp.int32)
    key_pos = first_pos - window + jnp.arange(ext_count, dtype=jnp.int32)
    allowed = (
        (key_pos[None, :] >= 0)
        & (key_pos[None, :] <= query_pos[:, None])
        & (key_pos[None, :] > query_pos[:, None] - window)
    )
    scores = jnp.where(allowed[None], scores, -jnp.inf)
    row_max = jnp.max(scores, axis=2, keepdims=True)
    log_total = row_max[:, :, 0] + jnp.log(jnp.sum(jnp.exp(scores - row_max), axis=2))
    probs = jnp.exp(scores - log_total[:, :, None])
    weights_low = probs.astype(jnp.bfloat16)
    output = jnp.einsum("hts,shd->thd", weights_low, values, preferred_element_type=jnp.float32)
    dprobs = jnp.einsum("thd,shd->hts", upstream, values, preferred_element_type=jnp.float32)
    row_dot = jnp.sum(probs * dprobs, axis=2)
    dscores = (probs * (dprobs - row_dot[:, :, None]) * score_scale).astype(jnp.bfloat16)
    query_grad = jnp.einsum("hts,shd->thd", dscores, keys, preferred_element_type=jnp.float32)
    return (output, query_grad, log_total, row_dot)


def key_head(query, upstream, totals, dots, keys, values, first_pos, total_rows):
    row_count = keys.shape[0]
    ext_count = query.shape[0]
    window = ext_count - row_count
    score_scale = 1.0 / math.sqrt(query.shape[2])
    scores = jnp.einsum("thd,shd->hts", query, keys, preferred_element_type=jnp.float32) * score_scale
    query_pos = first_pos + jnp.arange(ext_count, dtype=jnp.int32)
    key_pos = first_pos + jnp.arange(row_count, dtype=jnp.int32)
    allowed = (
        (query_pos[:, None] < total_rows)
        & (key_pos[None, :] <= query_pos[:, None])
        & (key_pos[None, :] > query_pos[:, None] - window)
    )
    probs = jnp.where(allowed[None], jnp.exp(scores - totals[:, :, None]), 0.0)
    weights_low = probs.astype(jnp.bfloat16)
    dprobs = jnp.einsum("thd,shd->hts", upstream, values, preferred_element_type=jnp.float32)
    dscores = (probs * (dprobs - dots[:, :, None]) * score_scale).astype(jnp.bfloat16)
    key_grad = jnp.einsum("hts,thd->shd", dscores, query, preferred_element_type=jnp.float32)
    value_grad = jnp.einsum("hts,thd->shd", weights_low, upstream, preferred_element_type=jnp.float32)
    return (key_grad, value_grad)


CTX = ("cy", "cz")


def shards(lin_q, lin_k, lin_v, win_q, win_k, win_v, grad_out):
    row_count = lin_q.shape[0]
    head_count = lin_q.shape[1] // HD
    shaped = (row_count, head_count, HD)
    flat = (row_count, head_count * HD)
    span = WIN // row_count
    total_rows = row_count * lax.axis_size(CTX[0]) * lax.axis_size(CTX[1])
    first_pos = lax.axis_index(CTX) * row_count
    win_query = win_q.reshape(shaped)
    win_key = win_k.reshape(shaped)
    win_value = win_v.reshape(shaped)
    cotangent = grad_out.reshape(shaped)

    earlier_keys, earlier_values = [], []
    later_queries, later_upstreams = [], []
    key_pair = jnp.stack([win_key, win_value])
    row_pair = jnp.stack([win_query, cotangent])
    for _ in range(span):
        key_pair = passed_along(key_pair, CTX, 1)
        row_pair = passed_along(row_pair, CTX, -1)
        earlier_keys.insert(0, key_pair[0])
        earlier_values.insert(0, key_pair[1])
        later_queries.append(row_pair[0])
        later_upstreams.append(row_pair[1])

    lin_query = lin_q.reshape(shaped)
    lin_key = lin_k.reshape(shaped)
    lin_value = lin_v.reshape(shaped)
    key_state = jnp.einsum("shd,she->hde", lin_key, lin_value, preferred_element_type=jnp.float32)
    prefix = scan_states(key_state, CTX[0], CTX[1], False)
    lin_out, lin_scores = linear_forward(lin_query, lin_key, lin_value, prefix)
    upstream = grad_out.reshape(shaped).astype(jnp.float32)
    square_sum, cross_sum = head_sum(
        jnp.stack([jnp.sum(lin_out * lin_out, axis=(1, 2)), jnp.sum(upstream * lin_out, axis=(1, 2))]),
        "head",
    )
    features = head_count * HD * lax.axis_size("head")
    inv_rms = lax.rsqrt(square_sum / features + NORM_EPS)
    lin_dout = (
        inv_rms[:, None, None] * upstream
        - lin_out * (inv_rms**3 * cross_sum / features)[:, None, None]
    ).astype(jnp.bfloat16)
    query_state = jnp.einsum(
        "thd,the->hde", lin_query, lin_dout, preferred_element_type=jnp.float32
    )
    suffix = scan_flat(query_state, CTX, True)
    grad_q, grad_k, grad_v = linear_backward(
        lin_query, lin_key, lin_value, lin_dout, lin_scores, prefix, suffix
    )

    key_ext = jnp.concatenate(earlier_keys + [win_key], axis=0)
    value_ext = jnp.concatenate(earlier_values + [win_value], axis=0)
    win_out, win_dq, log_total, row_dot = query_head(
        win_query, key_ext, value_ext, cotangent, first_pos
    )

    later_totals, later_dots = [], []
    stat_pair = jnp.stack([log_total, row_dot])
    for distance in range(1, span + 1):
        stat_pair = passed_along(jnp.stack([log_total, row_dot]), CTX, -distance)
        later_totals.append(stat_pair[0])
        later_dots.append(stat_pair[1])
    query_ext = jnp.concatenate([win_query] + later_queries, axis=0)
    upstream_ext = jnp.concatenate([cotangent] + later_upstreams, axis=0)
    total_ext = jnp.concatenate([log_total] + later_totals, axis=1)
    dot_ext = jnp.concatenate([row_dot] + later_dots, axis=1)
    win_dk, win_dv = key_head(
        query_ext, upstream_ext, total_ext, dot_ext, win_key, win_value, first_pos, total_rows
    )
    mixed = (lin_out * inv_rms[:, None, None] + win_out).astype(jnp.bfloat16).reshape(flat)
    return (
        mixed,
        grad_q.astype(jnp.bfloat16).reshape(flat),
        grad_k.astype(jnp.bfloat16).reshape(flat),
        grad_v.astype(jnp.bfloat16).reshape(flat),
        win_dq.astype(jnp.bfloat16).reshape(flat),
        win_dk.astype(jnp.bfloat16).reshape(flat),
        win_dv.astype(jnp.bfloat16).reshape(flat),
    )


def ctx_groups(mesh):
    column = list(mesh.devices[:, 0])
    count = len(column)
    try:
        slow = [tuple(d.coords)[1] for d in column]
    except (AttributeError, TypeError, IndexError):
        return 1, count
    inner = next((i for i, y in enumerate(slow) if y != slow[0]), count)
    if count % inner:
        inner = count
    return count // inner, inner


def solution(mesh):
    outer, inner = ctx_groups(mesh)
    heads = mesh.devices.shape[1]
    split = jax.sharding.Mesh(mesh.devices.reshape(outer, inner, heads), CTX + ("head",))
    spec = P(CTX, "head")
    return jax.shard_map(
        shards,
        mesh=split,
        in_specs=(spec,) * 7,
        out_specs=(spec,) * 7,
        check_vma=False,
    )
```
